32 devices in a mesh: group: 2 (over y), replica: 16 (over z, x, core).
Axes of the slice: x: 2, y: 2, z: 4, core: 2. Of those that a mesh axis runs over, the one named last changes fastest.
Arguments:
- tokens: bfloat16 [6144, 960], P(('group', 'replica')), may hold values from -6 to 6
- seq_lens: int32 [32, 4], P(('group', 'replica')), may hold values from 1 to 96, 192 in all within a row
- cotangent: bfloat16 [6144, 960], P(('group', 'replica')), may hold values from -6 to 6
- norm1_gain: bfloat16 [960], P('group'), may hold values from 0.25 to 1.75
- w_query: bfloat16 [960, 960], P('group'), may hold values from -0.1875 to 0.1875
- key_weight: bfloat16 [960, 320], P('group'), may hold values from -0.1875 to 0.1875
- value_weight: bfloat16 [960, 320], P('group'), may hold values from -0.1875 to 0.1875
- w_output: bfloat16 [960, 960], P('group'), may hold values from -0.5 to 0.5
- norm2_gain: bfloat16 [960], P('group'), may hold values from 0.25 to 1.75
- w_gate: bfloat16 [960, 2560], P(None, 'group'), may hold values from -0.1875 to 0.1875
- w_up: bfloat16 [960, 2560], P(None, 'group'), may hold values from -0.1875 to 0.1875
- w_down: bfloat16 [2560, 960], P('group'), may hold values from -0.125 to 0.125
Outputs:
- layer_out: bfloat16 [6144, 960], P(('group', 'replica'))
- tokens_grad: float32 [6144, 960], P(('group', 'replica'))
- norm1_gain_grad: float32 [960], P('group')
- w_query_grad: float32 [960, 960], P('group')
- w_key_grad: float32 [960, 320], P('group')
- w_value_grad: float32 [960, 320], P('group')
- w_output_grad: float32 [960, 960], P('group')
- norm2_gain_grad: float32 [960], P('group')
- w_gate_grad: float32 [960, 2560], P(None, 'group')
- w_up_grad: float32 [960, 2560], P(None, 'group')
- w_down_grad: float32 [2560, 960], P('group')
The draws below stay inside these ranges and needn't reach their ends.
Inputs may be any that keep to these rules, and one draw needn't show every extreme that they name: `seq_lens`: each device's row holds the lengths of its 4 sequences, which add up to 192; the longest in every row is 96.
All inputs are finite; a program needn't handle non-finite values.
Results may differ from the reference program's by a relative error of at most 0.023.
Values may be sent and summed in bfloat16 or wider, within the bound.
A program may use at most 192 MiB of HBM per device.

```python
import math
import jax
import jax.numpy as jnp
import numpy as np
from jax import lax

MODEL_WIDTH = 960
QUERY_HEADS = 15
KEY_VALUE_HEADS = 5
HEAD_SIZE = 64
FF = 2560
TOK_DEV = 192
SEQS_DEV = 4
SEQ_MAX = 96
TOKENS = 6144
N_GROUP = 2
N_REPLICA = 16


def levels(rng, shape, split, smallest, largest):
    def one(dim, parts):
        draws = jax.random.uniform(jax.random.fold_in(jax.random.fold_in(rng, 6), dim), (parts,), jnp.float32, smallest / len(split), largest / len(split))
        return jnp.repeat(jnp.exp(draws), shape[dim] // parts).reshape((-1,) + (1,) * (len(shape) - dim - 1))

    factor_of = one(*split[0])
    for cut in split[1:]:
        factor_of = factor_of * one(*cut)
    return factor_of


def profile(amount, total, limit, slope):
    loads = [(1 << 20) // math.isqrt(rank ** slope) + 1 for rank in range(2, amount + 1)]
    spare, given = total - limit - (amount - 1), [1] * (amount - 1)
    while spare > 0:
        movable = [i for i in range(amount - 1) if given[i] < limit]
        mass, budget = sum([loads[i] for i in movable]), spare
        for i in movable:
            extra = min(limit - given[i], max(1, budget * loads[i] // mass), spare)
            given[i] = given[i] + extra
            spare = spare - extra
    return np.array([limit] + given)


def ragged_sizes(stream_key, count, total, bound, lean):
    if count == 2:
        one = jax.random.randint(stream_key, (), max(1, total - bound), min(bound, total - 1) + 1)
        return jnp.stack([one, total - one])
    tallies = jnp.asarray(profile(count, total, bound, lean), jnp.int32)
    twos = (count - 1) // 2
    source_of, sink = tallies[1:1 + 2 * twos:2], tallies[2:2 + 2 * twos:2]
    room = jnp.minimum(source_of - 1, bound - sink)
    passed = jax.random.randint(jax.random.fold_in(stream_key, 1), (twos,), 0, 1 << 20) % (room + 1)
    tallies = tallies.at[1:1 + 2 * twos:2].set(source_of - passed).at[2:2 + 2 * twos:2].set(sink + passed)
    return tallies[jax.random.permutation(jax.random.fold_in(stream_key, 2), count)]


def normal_values(key, shape, deviation, limit, pieces=(), kind=jnp.bfloat16):
    drawn = deviation * jax.random.normal(key, shape, jnp.float32)
    if pieces:
        drawn = drawn * levels(key, shape, pieces, -0.22, 0.18)
    return jnp.clip(drawn, -limit, limit).astype(kind)


def setup_inputs(seed: int = 0) -> dict:
    splits = jax.random.split(jax.random.key(seed), 13)
    return {
        "tokens": normal_values(splits[0], (TOKENS, MODEL_WIDTH), 1.0, 6.0, ((0, 32),)),
        "seq_lens": jax.vmap(lambda own: ragged_sizes(own, SEQS_DEV, TOK_DEV, SEQ_MAX, 2))(jax.random.split(splits[1], (N_GROUP * N_REPLICA))).reshape((N_GROUP * N_REPLICA, SEQS_DEV)).astype(jnp.int32),
        "cotangent": normal_values(splits[2], (TOKENS, MODEL_WIDTH), 1.0, 6.0, ((0, 32),)),
        "norm1_gain": jnp.clip(1.0 + 0.15 * jax.random.normal(splits[3], (MODEL_WIDTH,), jnp.float32), 0.25, 1.75).astype(jnp.bfloat16),
        "w_query": normal_values(splits[4], (MODEL_WIDTH, QUERY_HEADS * HEAD_SIZE), MODEL_WIDTH ** -0.5, 0.1875, ((0, 2),)),
        "key_weight": normal_values(splits[5], (MODEL_WIDTH, KEY_VALUE_HEADS * HEAD_SIZE), MODEL_WIDTH ** -0.5, 0.1875, ((0, 2),)),
        "value_weight": normal_values(splits[6], (MODEL_WIDTH, KEY_VALUE_HEADS * HEAD_SIZE), MODEL_WIDTH ** -0.5, 0.1875, ((0, 2),)),
        "w_output": normal_values(splits[7], (QUERY_HEADS * HEAD_SIZE, MODEL_WIDTH), (QUERY_HEADS * HEAD_SIZE // 8) ** -0.5, 0.5, ((0, 2),)),
        "norm2_gain": jnp.clip(1.0 + 0.15 * jax.random.normal(splits[8], (MODEL_WIDTH,), jnp.float32), 0.25, 1.75).astype(jnp.bfloat16),
        "w_gate": normal_values(splits[9], (MODEL_WIDTH, FF), MODEL_WIDTH ** -0.5, 0.1875, ((1, 2),)),
        "w_up": normal_values(splits[10], (MODEL_WIDTH, FF), MODEL_WIDTH ** -0.5, 0.1875, ((1, 2),)),
        "w_down": normal_values(splits[11], (FF, MODEL_WIDTH), FF ** -0.5, 0.125, ((0, 2),)),
    }


EPS = 1e-05

def matrix_product(left, right):
    return jnp.dot(left, right, preferred_element_type=jnp.float32)

def left_t_product(left, right):
    return lax.dot_general(left, right, (((0,), (0,)), ((), ())), preferred_element_type=jnp.float32)

def right_t_product(left, right):
    return lax.dot_general(left, right, (((1,), (1,)), ((), ())), preferred_element_type=jnp.float32)

def wide_einsum(form, left, right):
    return jnp.einsum(form, left.astype(jnp.float32), right.astype(jnp.float32))

def sequence_tables(lengths, token_count):
    ends = jnp.cumsum(lengths).astype(jnp.int32)
    starts = ends - lengths
    indices = jnp.arange(token_count, dtype=jnp.int32)
    seq_of = lax.optimization_barrier(jnp.sum((indices[:, None] >= ends[None, :]).astype(jnp.int32), axis=1))
    onehot = (seq_of[:, None] == jnp.arange(lengths.shape[0], dtype=jnp.int32)[None, :]).astype(jnp.int32)
    position = indices - lax.optimization_barrier(jnp.sum(onehot * starts[None, :], axis=1))
    half_dim = HEAD_SIZE // 2
    freqs = 10000.0 ** (-(jnp.arange(half_dim, dtype=jnp.float32) * 2.0 / HEAD_SIZE))
    angles = position.astype(jnp.float32)[:, None] * freqs[None, :]
    visible = (seq_of[:, None] == seq_of[None, :]) & (indices[None, :] <= indices[:, None])
    return (jnp.cos(angles), jnp.sin(angles), visible)

def apply_rotary(values, cosine_table, sine_table):
    half_dim = values.shape[-1] // 2
    first_half = values[..., :half_dim]
    second_half = values[..., half_dim:]
    cos_b = cosine_table[:, None, :]
    sin_b = sine_table[:, None, :]
    return jnp.concatenate([first_half * cos_b - second_half * sin_b, second_half * cos_b + first_half * sin_b], axis=-1)

def rotary_backward(values, cosine_table, sine_table):
    half_dim = values.shape[-1] // 2
    first_half = values[..., :half_dim]
    second_half = values[..., half_dim:]
    cos_b = cosine_table[:, None, :]
    sin_b = sine_table[:, None, :]
    return jnp.concatenate([first_half * cos_b + second_half * sin_b, second_half * cos_b - first_half * sin_b], axis=-1)

def rms_scale(resid, gain):
    inv_rms = lax.rsqrt(lax.optimization_barrier(jnp.mean(resid * resid, axis=-1, keepdims=True)) + EPS)
    return ((resid * inv_rms * gain.astype(jnp.float32)).astype(jnp.bfloat16), inv_rms)

def rms_back(d_normed, resid, inv_rms, gain):
    scaled = d_normed * gain.astype(jnp.float32)
    d_resid = inv_rms * scaled - resid * inv_rms ** 3 * lax.optimization_barrier(jnp.mean(scaled * resid, axis=-1, keepdims=True))
    d_gain = lax.optimization_barrier(jnp.sum(d_normed * resid * inv_rms, axis=0))
    return (d_resid, d_gain)

def masked_scores(query_rotated, key_rotated, visible):
    token_count = query_rotated.shape[0]
    query_grouped = query_rotated.reshape(token_count, KEY_VALUE_HEADS, QUERY_HEADS // KEY_VALUE_HEADS, HEAD_SIZE)
    scores = wide_einsum('qhgd,khd->hgqk', query_grouped, key_rotated) * (1.0 / math.sqrt(HEAD_SIZE))
    return (jnp.where(visible[None, None], scores, -1e+30), query_grouped)

def attention(query_rotated, key_rotated, value_row_block, visible):
    token_count = query_rotated.shape[0]
    scores, query_grouped = masked_scores(query_rotated, key_rotated, visible)
    top = lax.optimization_barrier(jnp.max(scores, axis=-1, keepdims=True))
    expo = jnp.exp(scores - top)
    total = lax.optimization_barrier(jnp.sum(expo, axis=-1, keepdims=True))
    log_total = top + jnp.log(total)
    probs = (expo / total).astype(jnp.bfloat16)
    mixed = wide_einsum('hgqk,khd->qhgd', probs, value_row_block)
    return (mixed.reshape(token_count, QUERY_HEADS * HEAD_SIZE).astype(jnp.bfloat16), log_total)

def attention_back(query_rotated, key_rotated, value_row_block, attention_mixture, mixture_gradient, log_total, visible):
    token_count = query_rotated.shape[0]
    scores, query_grouped = masked_scores(query_rotated, key_rotated, visible)
    weights_f = jnp.exp(scores - log_total)
    probs = weights_f.astype(jnp.bfloat16)
    mixture_gradient_grouped = mixture_gradient.reshape(token_count, KEY_VALUE_HEADS, QUERY_HEADS // KEY_VALUE_HEADS, HEAD_SIZE)
    mixture_grouped = attention_mixture.reshape(token_count, KEY_VALUE_HEADS, QUERY_HEADS // KEY_VALUE_HEADS, HEAD_SIZE)
    value_gradient = wide_einsum('hgqk,qhgd->khd', probs, mixture_gradient_grouped)
    d_probs = wide_einsum('qhgd,khd->hgqk', mixture_gradient_grouped, value_row_block)
    delta = wide_einsum('qhgd,qhgd->hgq', mixture_gradient_grouped, mixture_grouped)[..., None]
    d_scores = (weights_f * (d_probs - delta) * (1.0 / math.sqrt(HEAD_SIZE))).astype(jnp.bfloat16)
    d_query = wide_einsum('hgqk,khd->qhgd', d_scores, key_rotated).reshape(token_count, QUERY_HEADS, HEAD_SIZE)
    key_gradient = wide_einsum('hgqk,qhgd->khd', d_scores, query_grouped)
    return (d_query, key_gradient, value_gradient)

def forward_pass(block, lengths, weights):
    gain_one, w_query, key_weight, value_weight, w_output, gain_two, w_gate, w_up, w_down = weights
    token_count = block.shape[0]
    cosine_table, sine_table, visible = sequence_tables(lengths, token_count)
    resid_in = block.astype(jnp.float32)
    first_normed_input, inv_rms_one = rms_scale(resid_in, gain_one)
    query_rotated = apply_rotary(matrix_product(first_normed_input, w_query).reshape(token_count, QUERY_HEADS, HEAD_SIZE), cosine_table, sine_table).astype(jnp.bfloat16)
    key_rotated = apply_rotary(matrix_product(first_normed_input, key_weight).reshape(token_count, KEY_VALUE_HEADS, HEAD_SIZE), cosine_table, sine_table).astype(jnp.bfloat16)
    value_row_block = matrix_product(first_normed_input, value_weight).astype(jnp.bfloat16).reshape(token_count, KEY_VALUE_HEADS, HEAD_SIZE)
    attention_mixture, log_total = attention(query_rotated, key_rotated, value_row_block, visible)
    resid_mid = resid_in + matrix_product(attention_mixture, w_output)
    normed_two, inv_rms_two = rms_scale(resid_mid, gain_two)
    gate_pre = matrix_product(normed_two, w_gate)
    up_pre = matrix_product(normed_two, w_up)
    hidden = (jax.nn.silu(gate_pre) * up_pre).astype(jnp.bfloat16)
    resid_out = resid_mid + matrix_product(hidden, w_down)
    saved = (resid_in, first_normed_input, inv_rms_one, query_rotated, key_rotated, value_row_block, attention_mixture, log_total, resid_mid, normed_two, inv_rms_two, gate_pre, up_pre, hidden, cosine_table, sine_table, visible)
    return (resid_out.astype(jnp.bfloat16), saved)

def mlp_backward(d_out, saved, weights):
    gain_one, w_query, key_weight, value_weight, w_output, gain_two, w_gate, w_up, w_down = weights
    resid_mid, normed_two, inv_rms_two, gate_pre, up_pre, hidden = saved[8:14]
    d_out_b = d_out.astype(jnp.bfloat16)
    grad_down = left_t_product(hidden, d_out_b)
    d_hidden = right_t_product(d_out_b, w_down)
    sigma = jax.nn.sigmoid(gate_pre)
    d_gate = (d_hidden * up_pre * sigma * (1.0 + gate_pre * (1.0 - sigma))).astype(jnp.bfloat16)
    d_up = (d_hidden * gate_pre * sigma).astype(jnp.bfloat16)
    grad_gate = left_t_product(normed_two, d_gate)
    grad_up = left_t_product(normed_two, d_up)
    d_normed_two = right_t_product(d_gate, w_gate) + right_t_product(d_up, w_up)
    d_resid_part, grad_gain_two = rms_back(d_normed_two, resid_mid, inv_rms_two, gain_two)
    return (d_out + d_resid_part, (grad_gain_two, grad_gate, grad_up, grad_down))

def attn_backward(d_resid_mid, saved, weights):
    gain_one, w_query, key_weight, value_weight, w_output, gain_two, w_gate, w_up, w_down = weights
    resid_in, first_normed_input, inv_rms_one, query_rotated, key_rotated, value_row_block, attention_mixture, log_total = saved[:8]
    cosine_table, sine_table, visible = saved[14:]
    token_count = resid_in.shape[0]
    d_mid_b = d_resid_mid.astype(jnp.bfloat16)
    grad_output = left_t_product(attention_mixture, d_mid_b)
    mixture_gradient = right_t_product(d_mid_b, w_output).astype(jnp.bfloat16)
    d_query, key_gradient, value_gradient = attention_back(query_rotated, key_rotated, value_row_block, attention_mixture, mixture_gradient, log_total, visible)
    d_query_b = rotary_backward(d_query, cosine_table, sine_table).reshape(token_count, QUERY_HEADS * HEAD_SIZE).astype(jnp.bfloat16)
    key_gradient_block = rotary_backward(key_gradient, cosine_table, sine_table).reshape(token_count, KEY_VALUE_HEADS * HEAD_SIZE).astype(jnp.bfloat16)
    value_gradient_block = value_gradient.reshape(token_count, KEY_VALUE_HEADS * HEAD_SIZE).astype(jnp.bfloat16)
    grad_query = left_t_product(first_normed_input, d_query_b)
    grad_key = left_t_product(first_normed_input, key_gradient_block)
    grad_value = left_t_product(first_normed_input, value_gradient_block)
    d_normed_one = right_t_product(d_query_b, w_query) + right_t_product(key_gradient_block, key_weight) + right_t_product(value_gradient_block, value_weight)
    d_resid_part, grad_gain_one = rms_back(d_normed_one, resid_in, inv_rms_one, gain_one)
    return (d_resid_mid + d_resid_part, (grad_gain_one, grad_query, grad_key, grad_value, grad_output))

def reference(tokens, seq_lens, cotangent, norm1_gain, w_query, key_weight, value_weight, w_output, norm2_gain, w_gate, w_up, w_down):
    weights = (norm1_gain, w_query, key_weight, value_weight, w_output, norm2_gain, w_gate, w_up, w_down)
    blocks = N_GROUP * N_REPLICA
    token_blocks = tokens.reshape(blocks, TOK_DEV, MODEL_WIDTH)
    cot_blocks = cotangent.reshape(blocks, TOK_DEV, MODEL_WIDTH)
    zeros = tuple((jnp.zeros(weight.shape, jnp.float32) for weight in weights))

    def step(totals, item):
        block, lengths, cot_block = item
        layer_block, saved = forward_pass(block, lengths, weights)
        d_resid_mid, mlp_grads = mlp_backward(cot_block.astype(jnp.float32), saved, weights)
        d_tokens, attn_grads = attn_backward(d_resid_mid, saved, weights)
        grads = attn_grads + mlp_grads
        rounded = tuple((lax.optimization_barrier(part.astype(jnp.bfloat16)).astype(jnp.float32) for part in grads))
        return (tuple((total + part for total, part in zip(totals, rounded))), (layer_block, d_tokens))
    totals, (outs, d_tokens) = lax.scan(step, zeros, (token_blocks, seq_lens, cot_blocks))
    factor = 1.0 / math.sqrt(float(TOKENS))
    return (outs.reshape(TOKENS, MODEL_WIDTH), d_tokens.reshape(TOKENS, MODEL_WIDTH), totals[0] * factor, totals[1] * factor, totals[2] * factor, totals[3] * factor, totals[4] * factor, totals[5] * factor, totals[6] * factor, totals[7] * factor, totals[8] * factor)
```

```python
import math

import jax
import jax.numpy as jnp
from jax import lax
from jax.sharding import PartitionSpec as P

QUERY_HEADS = 15
KEY_VALUE_HEADS = 5
HEAD_SIZE = 64


EPS = 1e-05


def matrix_product(left, right):
    return jnp.dot(left, right, preferred_element_type=jnp.float32)


def left_t_product(left, right):
    return lax.dot_general(
        left, right, (((0,), (0,)), ((), ())), preferred_element_type=jnp.float32
    )


def right_t_product(left, right):
    return lax.dot_general(
        left, right, (((1,), (1,)), ((), ())), preferred_element_type=jnp.float32
    )


def mixed_einsum(form, left, right):
    return jnp.einsum(form, left, right, preferred_element_type=jnp.float32)


def sequence_tables(lengths, token_count):
    ends = jnp.cumsum(lengths)
    starts = ends - lengths
    indices = jnp.arange(token_count, dtype=jnp.int32)
    seq_of = jnp.sum((indices[:, None] >= ends[None, :]).astype(jnp.int32), axis=1)
    onehot = (seq_of[:, None] == jnp.arange(lengths.shape[0], dtype=jnp.int32)[None, :]).astype(
        jnp.int32
    )
    position = indices - jnp.sum(onehot * starts[None, :], axis=1)
    half_dim = HEAD_SIZE // 2
    freqs = 10000.0 ** (-(jnp.arange(half_dim, dtype=jnp.float32) * 2.0 / HEAD_SIZE))
    angles = position.astype(jnp.float32)[:, None] * freqs[None, :]
    visible = (seq_of[:, None] == seq_of[None, :]) & (indices[None, :] <= indices[:, None])
    return (jnp.cos(angles), jnp.sin(angles), visible)


def apply_rotary(values, cosine_table, sine_table):
    half_dim = values.shape[-1] // 2
    first_half = values[..., :half_dim]
    second_half = values[..., half_dim:]
    cos_b = cosine_table[:, None, :]
    sin_b = sine_table[:, None, :]
    return jnp.concatenate(
        [first_half * cos_b - second_half * sin_b, second_half * cos_b + first_half * sin_b],
        axis=-1,
    )


def rotary_backward(values, cosine_table, sine_table):
    half_dim = values.shape[-1] // 2
    first_half = values[..., :half_dim]
    second_half = values[..., half_dim:]
    cos_b = cosine_table[:, None, :]
    sin_b = sine_table[:, None, :]
    return jnp.concatenate(
        [first_half * cos_b + second_half * sin_b, second_half * cos_b - first_half * sin_b],
        axis=-1,
    )


def rms_scale(resid, gain):
    inv_rms = lax.rsqrt(jnp.mean(resid * resid, axis=-1, keepdims=True) + EPS)
    return ((resid * inv_rms * gain.astype(jnp.float32)).astype(jnp.bfloat16), inv_rms)


def rms_back(d_normed, resid, inv_rms, gain):
    scaled = d_normed * gain.astype(jnp.float32)
    d_resid = inv_rms * scaled - resid * inv_rms**3 * jnp.mean(
        scaled * resid, axis=-1, keepdims=True
    )
    d_gain = jnp.sum(d_normed * resid * inv_rms, axis=0)
    return (d_resid, d_gain)


def masked_scores(query_rotated, key_rotated, visible):
    token_count = query_rotated.shape[0]
    query_grouped = query_rotated.reshape(
        token_count, KEY_VALUE_HEADS, QUERY_HEADS // KEY_VALUE_HEADS, HEAD_SIZE
    )
    scores = mixed_einsum("qhgd,khd->hgqk", query_grouped, key_rotated) * (
        1.0 / math.sqrt(HEAD_SIZE)
    )
    return (jnp.where(visible[None, None], scores, -1e30), query_grouped)


def attention(query_rotated, key_rotated, value_row_block, visible):
    token_count = query_rotated.shape[0]
    scores, query_grouped = masked_scores(query_rotated, key_rotated, visible)
    top = jnp.max(scores, axis=-1, keepdims=True)
    expo = jnp.exp(scores - top)
    total = jnp.sum(expo, axis=-1, keepdims=True)
    log_total = top + jnp.log(total)
    probs = (expo / total).astype(jnp.bfloat16)
    mixed = mixed_einsum("hgqk,khd->qhgd", probs, value_row_block)
    return (mixed.reshape(token_count, QUERY_HEADS * HEAD_SIZE).astype(jnp.bfloat16), log_total)


def attention_back(
    query_rotated,
    key_rotated,
    value_row_block,
    attention_mixture,
    mixture_gradient,
    log_total,
    visible,
):
    token_count = query_rotated.shape[0]
    scores, query_grouped = masked_scores(query_rotated, key_rotated, visible)
    weights_f = jnp.exp(scores - log_total)
    probs = weights_f.astype(jnp.bfloat16)
    mixture_gradient_grouped = mixture_gradient.reshape(
        token_count, KEY_VALUE_HEADS, QUERY_HEADS // KEY_VALUE_HEADS, HEAD_SIZE
    )
    mixture_grouped = attention_mixture.reshape(
        token_count, KEY_VALUE_HEADS, QUERY_HEADS // KEY_VALUE_HEADS, HEAD_SIZE
    )
    value_gradient = mixed_einsum("hgqk,qhgd->khd", probs, mixture_gradient_grouped)
    d_probs = mixed_einsum("qhgd,khd->hgqk", mixture_gradient_grouped, value_row_block)
    delta = mixed_einsum("qhgd,qhgd->hgq", mixture_gradient_grouped, mixture_grouped)[..., None]
    d_scores = (weights_f * (d_probs - delta) * (1.0 / math.sqrt(HEAD_SIZE))).astype(jnp.bfloat16)
    d_query = mixed_einsum("hgqk,khd->qhgd", d_scores, key_rotated).reshape(
        token_count, QUERY_HEADS, HEAD_SIZE
    )
    key_gradient = mixed_einsum("hgqk,qhgd->khd", d_scores, query_grouped)
    return (d_query, key_gradient, value_gradient)


def from_member(values, shift):
    size = lax.axis_size("group")
    return lax.ppermute(values, "group", [(j, (j - shift) % size) for j in range(size)])


def to_member(values, shift):
    size = lax.axis_size("group")
    return lax.ppermute(values, "group", [(j, (j + shift) % size) for j in range(size)])


def group_tokens(values):
    others = [from_member(values, k) for k in range(1, lax.axis_size("group"))]
    return jnp.concatenate([values] + others, axis=0)


def group_scatter_sum(parts, token_count):
    total = parts[:token_count]
    for k in range(1, lax.axis_size("group")):
        part = parts[k * token_count : (k + 1) * token_count].astype(jnp.bfloat16)
        total = total + to_member(part, k).astype(jnp.float32)
    return total


def in_group_order(blocks, axis):
    size = len(blocks)
    me = lax.axis_index("group")
    if size == 2:
        first = jnp.where(me == 0, blocks[0], blocks[1])
        second = jnp.where(me == 0, blocks[1], blocks[0])
        return jnp.concatenate([first, second], axis=axis)
    stacked = jnp.roll(jnp.stack(blocks), me, axis=0)
    return jnp.concatenate([stacked[i] for i in range(size)], axis=axis)


def gather_rows(block):
    half = block.shape[0] // 2
    core = lax.rem(lax.axis_index("replica"), 2)
    pairs = [(i, i ^ 1) for i in range(lax.axis_size("replica"))]
    mine = lax.dynamic_slice_in_dim(block, core * half, half, axis=0)
    blocks = [block]
    for k in range(1, lax.axis_size("group")):
        piece = from_member(mine, k)
        pair = lax.ppermute(piece, "replica", pairs)
        first = jnp.where(core == 0, piece, pair)
        second = jnp.where(core == 0, pair, piece)
        blocks.append(jnp.concatenate([first, second], axis=0))
    return in_group_order(blocks, 0)


def partner(values, bit):
    size = lax.axis_size("replica")
    return lax.ppermute(values, "replica", [(i, i ^ (1 << bit)) for i in range(size)])


def upper_half(bit):
    return (lax.axis_index("replica") >> bit) & 1


def add_rounded(left, right):
    return (left.astype(jnp.float32) + right.astype(jnp.float32)).astype(jnp.bfloat16)


def halve(values, bit, axis=0):
    half = values.shape[axis] // 2
    upper = upper_half(bit)
    kept = lax.dynamic_slice_in_dim(values, upper * half, half, axis=axis)
    sent = lax.dynamic_slice_in_dim(values, (1 - upper) * half, half, axis=axis)
    return add_rounded(kept, partner(sent, bit))


def rejoin(values, bit):
    other = partner(values, bit)
    lower = upper_half(bit) == 0
    return jnp.concatenate(
        [jnp.where(lower, values, other), jnp.where(lower, other, values)], axis=0
    )


def bit_order(swapped):
    bits = list(range(int(math.log2(lax.axis_size("replica")))))
    if swapped and len(bits) > 2:
        bits[1], bits[2] = bits[2], bits[1]
    return bits


def replica_sum(values, swapped):
    bits = bit_order(swapped)
    for bit in bits:
        values = halve(values, bit)
    for bit in reversed(bits):
        values = rejoin(values, bit)
    return values


def local(
    tokens,
    seq_lens,
    cotangent,
    norm1_gain,
    w_query,
    key_weight,
    value_weight,
    w_output,
    norm2_gain,
    w_gate,
    w_up,
    w_down,
):
    token_count, width = tokens.shape
    group = lax.axis_index("group")
    half_width = w_query.shape[0]
    query_width = w_query.shape[1]
    key_width = key_weight.shape[1]
    gains_mine = jnp.stack([norm1_gain, norm2_gain])
    group_size = lax.axis_size("group")
    gains = in_group_order(
        [gains_mine] + [from_member(gains_mine, k) for k in range(1, group_size)], 1
    )
    gain_one, gain_two = gains[0], gains[1]
    qkv_weight = gather_rows(jnp.concatenate([w_query, key_weight, value_weight], axis=1))
    out_weight = gather_rows(w_output)
    d_out = cotangent.astype(jnp.float32)
    d_out_pair = group_tokens(cotangent)

    cosine_table, sine_table, visible = sequence_tables(seq_lens[0], token_count)
    resid_in = tokens.astype(jnp.float32)
    normed_one, inv_rms_one = rms_scale(resid_in, gain_one)
    qkv = matrix_product(normed_one, qkv_weight)
    query_rotated = apply_rotary(
        qkv[:, :query_width].reshape(token_count, QUERY_HEADS, HEAD_SIZE), cosine_table, sine_table
    ).astype(jnp.bfloat16)
    key_rotated = apply_rotary(
        qkv[:, query_width : query_width + key_width].reshape(
            token_count, KEY_VALUE_HEADS, HEAD_SIZE
        ),
        cosine_table,
        sine_table,
    ).astype(jnp.bfloat16)
    value_rows = (
        qkv[:, query_width + key_width :]
        .astype(jnp.bfloat16)
        .reshape(token_count, KEY_VALUE_HEADS, HEAD_SIZE)
    )
    attn_mix, log_total = attention(query_rotated, key_rotated, value_rows, visible)
    resid_mid = resid_in + matrix_product(attn_mix, out_weight)
    normed_two, inv_rms_two = rms_scale(resid_mid, gain_two)

    normed_pair = group_tokens(normed_two)
    gate_pre = matrix_product(normed_pair, w_gate)
    up_pre = matrix_product(normed_pair, w_up)
    sigma = jax.nn.sigmoid(gate_pre)
    hidden = (gate_pre * sigma * up_pre).astype(jnp.bfloat16)
    grad_down = left_t_product(hidden, d_out_pair).astype(jnp.bfloat16)
    sum_down = replica_sum(grad_down, False)
    d_hidden = right_t_product(d_out_pair, w_down)
    d_gate = (d_hidden * up_pre * sigma * (1.0 + gate_pre * (1.0 - sigma))).astype(jnp.bfloat16)
    d_up = (d_hidden * gate_pre * sigma).astype(jnp.bfloat16)
    d_normed_part = right_t_product(d_gate, w_gate) + right_t_product(d_up, w_up)
    d_normed_two = group_scatter_sum(d_normed_part, token_count)
    grad_gate = left_t_product(normed_pair, d_gate).astype(jnp.bfloat16)
    grad_up = left_t_product(normed_pair, d_up).astype(jnp.bfloat16)
    sum_gate = replica_sum(grad_gate, False)
    sum_up = replica_sum(grad_up, True)
    down_part = matrix_product(hidden, w_down)
    layer_out = (resid_mid + group_scatter_sum(down_part, token_count)).astype(jnp.bfloat16)

    d_resid_part, grad_gain_two = rms_back(d_normed_two, resid_mid, inv_rms_two, gain_two)
    d_resid_mid = d_out + d_resid_part
    d_mid_b = d_resid_mid.astype(jnp.bfloat16)
    grad_output = left_t_product(attn_mix, d_mid_b)
    d_mix = right_t_product(d_mid_b, out_weight).astype(jnp.bfloat16)
    d_query, d_key, d_value = attention_back(
        query_rotated, key_rotated, value_rows, attn_mix, d_mix, log_total, visible
    )
    d_qkv = jnp.concatenate(
        [
            rotary_backward(d_query, cosine_table, sine_table)
            .reshape(token_count, query_width)
            .astype(jnp.bfloat16),
            rotary_backward(d_key, cosine_table, sine_table)
            .reshape(token_count, key_width)
            .astype(jnp.bfloat16),
            d_value.reshape(token_count, key_width).astype(jnp.bfloat16),
        ],
        axis=1,
    )
    grad_qkv = left_t_product(normed_one, d_qkv)
    d_normed_one = right_t_product(d_qkv, qkv_weight)
    d_resid_first, grad_gain_one = rms_back(d_normed_one, resid_in, inv_rms_one, gain_one)
    tokens_grad = d_resid_mid + d_resid_first

    columns = query_width + 2 * key_width + width
    attn_grads = jnp.concatenate([grad_qkv, grad_output], axis=1).astype(jnp.bfloat16)
    replicas = lax.axis_size("replica")
    extra = replicas - half_width % replicas
    gain_rows = jnp.stack([grad_gain_one, grad_gain_two]).reshape(2, group_size, half_width)
    gain_rows = gain_rows.transpose(1, 0, 2).reshape(group_size, 1, 2 * half_width)
    gain_rows = jnp.pad(
        gain_rows.astype(jnp.bfloat16), ((0, 0), (0, extra - 1), (0, columns - 2 * half_width))
    )
    blocks = jnp.concatenate(
        [attn_grads.reshape(group_size, half_width, columns), gain_rows], axis=1
    )
    blocks = halve(blocks, 0, axis=1)
    summed = lax.dynamic_index_in_dim(blocks, group, axis=0, keepdims=False)
    for k in range(1, group_size):
        owner = lax.rem(group + k, group_size)
        part = lax.dynamic_index_in_dim(blocks, owner, axis=0, keepdims=False)
        summed = add_rounded(summed, to_member(part, k))
    later = bit_order(True)[1:]
    for bit in later:
        summed = halve(summed, bit)
    for bit in reversed(later):
        summed = rejoin(summed, bit)
    sum_attn = rejoin(summed, 0)

    factor = 1.0 / math.sqrt(
        float(token_count * lax.axis_size("group") * lax.axis_size("replica"))
    )

    def scaled(values):
        return values.astype(jnp.float32) * factor

    gain_sums = scaled(sum_attn[half_width])
    sum_attn = scaled(sum_attn[:half_width])
    return (
        layer_out,
        tokens_grad,
        gain_sums[:half_width],
        sum_attn[:, :query_width],
        sum_attn[:, query_width : query_width + key_width],
        sum_attn[:, query_width + key_width : query_width + 2 * key_width],
        sum_attn[:, query_width + 2 * key_width :],
        gain_sums[half_width : 2 * half_width],
        scaled(sum_gate),
        scaled(sum_up),
        scaled(sum_down),
    )


def solution(mesh):
    in_specs = (
        P(("group", "replica"), None),
        P(("group", "replica"), None),
        P(("group", "replica"), None),
        P("group"),
        P("group", None),
        P("group", None),
        P("group", None),
        P("group", None),
        P("group"),
        P(None, "group"),
        P(None, "group"),
        P("group", None),
    )
    out_specs = (
        P(("group", "replica"), None),
        P(("group", "replica"), None),
        P("group"),
        P("group", None),
        P("group", None),
        P("group", None),
        P("group", None),
        P("group"),
        P(None, "group"),
        P(None, "group"),
        P("group", None),
    )
    return jax.shard_map(local, mesh=mesh, in_specs=in_specs, out_specs=out_specs, check_vma=False)
```

```python
import math

import jax
import jax.numpy as jnp
from jax import lax
from jax.sharding import PartitionSpec as P

QUERY_HEADS = 15
KEY_VALUE_HEADS = 5
HEAD_SIZE = 64


EPS = 1e-05


def matrix_product(left, right):
    return jnp.dot(left, right, preferred_element_type=jnp.float32)


def left_t_product(left, right):
    return lax.dot_general(
        left, right, (((0,), (0,)), ((), ())), preferred_element_type=jnp.float32
    )


def right_t_product(left, right):
    return lax.dot_general(
        left, right, (((1,), (1,)), ((), ())), preferred_element_type=jnp.float32
    )


def mixed_einsum(form, left, right):
    return jnp.einsum(form, left, right, preferred_element_type=jnp.float32)


def sequence_tables(lengths, token_count):
    ends = jnp.cumsum(lengths)
    starts = ends - lengths
    indices = jnp.arange(token_count, dtype=jnp.int32)
    seq_of = jnp.sum((indices[:, None] >= ends[None, :]).astype(jnp.int32), axis=1)
    onehot = (seq_of[:, None] == jnp.arange(lengths.shape[0], dtype=jnp.int32)[None, :]).astype(
        jnp.int32
    )
    position = indices - jnp.sum(onehot * starts[None, :], axis=1)
    half_dim = HEAD_SIZE // 2
    freqs = 10000.0 ** (-(jnp.arange(half_dim, dtype=jnp.float32) * 2.0 / HEAD_SIZE))
    angles = position.astype(jnp.float32)[:, None] * freqs[None, :]
    visible = (seq_of[:, None] == seq_of[None, :]) & (indices[None, :] <= indices[:, None])
    return (jnp.cos(angles), jnp.sin(angles), visible)


def apply_rotary(values, cosine_table, sine_table):
    half_dim = values.shape[-1] // 2
    first_half = values[..., :half_dim]
    second_half = values[..., half_dim:]
    cos_b = cosine_table[:, None, :]
    sin_b = sine_table[:, None, :]
    return jnp.concatenate(
        [first_half * cos_b - second_half * sin_b, second_half * cos_b + first_half * sin_b],
        axis=-1,
    )


def rotary_backward(values, cosine_table, sine_table):
    half_dim = values.shape[-1] // 2
    first_half = values[..., :half_dim]
    second_half = values[..., half_dim:]
    cos_b = cosine_table[:, None, :]
    sin_b = sine_table[:, None, :]
    return jnp.concatenate(
        [first_half * cos_b + second_half * sin_b, second_half * cos_b - first_half * sin_b],
        axis=-1,
    )


def rms_scale(resid, gain):
    inv_rms = lax.rsqrt(jnp.mean(resid * resid, axis=-1, keepdims=True) + EPS)
    return ((resid * inv_rms * gain.astype(jnp.float32)).astype(jnp.bfloat16), inv_rms)


def rms_back(d_normed, resid, inv_rms, gain):
    scaled = d_normed * gain.astype(jnp.float32)
    d_resid = inv_rms * scaled - resid * inv_rms**3 * jnp.mean(
        scaled * resid, axis=-1, keepdims=True
    )
    d_gain = jnp.sum(d_normed * resid * inv_rms, axis=0)
    return (d_resid, d_gain)


def masked_scores(query_rotated, key_rotated, visible):
    token_count = query_rotated.shape[0]
    query_grouped = query_rotated.reshape(
        token_count, KEY_VALUE_HEADS, QUERY_HEADS // KEY_VALUE_HEADS, HEAD_SIZE
    )
    scores = mixed_einsum("qhgd,khd->hgqk", query_grouped, key_rotated) * (
        1.0 / math.sqrt(HEAD_SIZE)
    )
    return (jnp.where(visible[None, None], scores, -1e30), query_grouped)


def attention(query_rotated, key_rotated, value_row_block, visible):
    token_count = query_rotated.shape[0]
    scores, query_grouped = masked_scores(query_rotated, key_rotated, visible)
    top = jnp.max(scores, axis=-1, keepdims=True)
    expo = jnp.exp(scores - top)
    total = jnp.sum(expo, axis=-1, keepdims=True)
    log_total = top + jnp.log(total)
    probs = (expo / total).astype(jnp.bfloat16)
    mixed = mixed_einsum("hgqk,khd->qhgd", probs, value_row_block)
    return (mixed.reshape(token_count, QUERY_HEADS * HEAD_SIZE).astype(jnp.bfloat16), log_total)


def attention_back(
    query_rotated,
    key_rotated,
    value_row_block,
    attention_mixture,
    mixture_gradient,
    log_total,
    visible,
):
    token_count = query_rotated.shape[0]
    scores, query_grouped = masked_scores(query_rotated, key_rotated, visible)
    weights_f = jnp.exp(scores - log_total)
    probs = weights_f.astype(jnp.bfloat16)
    mixture_gradient_grouped = mixture_gradient.reshape(
        token_count, KEY_VALUE_HEADS, QUERY_HEADS // KEY_VALUE_HEADS, HEAD_SIZE
    )
    mixture_grouped = attention_mixture.reshape(
        token_count, KEY_VALUE_HEADS, QUERY_HEADS // KEY_VALUE_HEADS, HEAD_SIZE
    )
    value_gradient = mixed_einsum("hgqk,qhgd->khd", probs, mixture_gradient_grouped)
    d_probs = mixed_einsum("qhgd,khd->hgqk", mixture_gradient_grouped, value_row_block)
    delta = mixed_einsum("qhgd,qhgd->hgq", mixture_gradient_grouped, mixture_grouped)[..., None]
    d_scores = (weights_f * (d_probs - delta) * (1.0 / math.sqrt(HEAD_SIZE))).astype(jnp.bfloat16)
    d_query = mixed_einsum("hgqk,khd->qhgd", d_scores, key_rotated).reshape(
        token_count, QUERY_HEADS, HEAD_SIZE
    )
    key_gradient = mixed_einsum("hgqk,qhgd->khd", d_scores, query_grouped)
    return (d_query, key_gradient, value_gradient)


def from_member(values, shift):
    size = lax.axis_size("group")
    return lax.ppermute(values, "group", [(j, (j - shift) % size) for j in range(size)])


def to_member(values, shift):
    size = lax.axis_size("group")
    return lax.ppermute(values, "group", [(j, (j + shift) % size) for j in range(size)])


def group_tokens(values):
    others = [from_member(values, k) for k in range(1, lax.axis_size("group"))]
    return jnp.concatenate([values] + others, axis=0)


def group_scatter_sum(parts, token_count):
    total = parts[:token_count]
    for k in range(1, lax.axis_size("group")):
        part = parts[k * token_count : (k + 1) * token_count].astype(jnp.bfloat16)
        total = total + to_member(part, k).astype(jnp.float32)
    return total


def in_group_order(blocks, axis):
    size = len(blocks)
    me = lax.axis_index("group")
    if size == 2:
        first = jnp.where(me == 0, blocks[0], blocks[1])
        second = jnp.where(me == 0, blocks[1], blocks[0])
        return jnp.concatenate([first, second], axis=axis)
    stacked = jnp.roll(jnp.stack(blocks), me, axis=0)
    return jnp.concatenate([stacked[i] for i in range(size)], axis=axis)


def gather_rows(block):
    half = block.shape[0] // 2
    core = lax.rem(lax.axis_index("replica"), 2)
    pairs = [(i, i ^ 1) for i in range(lax.axis_size("replica"))]
    mine = lax.dynamic_slice_in_dim(block, core * half, half, axis=0)
    blocks = [block]
    for k in range(1, lax.axis_size("group")):
        piece = from_member(mine, k)
        pair = lax.ppermute(piece, "replica", pairs)
        first = jnp.where(core == 0, piece, pair)
        second = jnp.where(core == 0, pair, piece)
        blocks.append(jnp.concatenate([first, second], axis=0))
    return in_group_order(blocks, 0)


def partner(values, bit):
    size = lax.axis_size("replica")
    return lax.ppermute(values, "replica", [(i, i ^ (1 << bit)) for i in range(size)])


def upper_half(bit):
    return (lax.axis_index("replica") >> bit) & 1


def add_rounded(left, right):
    return (left.astype(jnp.float32) + right.astype(jnp.float32)).astype(jnp.bfloat16)


def halve(values, bit, axis=0):
    half = values.shape[axis] // 2
    upper = upper_half(bit)
    kept = lax.dynamic_slice_in_dim(values, upper * half, half, axis=axis)
    sent = lax.dynamic_slice_in_dim(values, (1 - upper) * half, half, axis=axis)
    return add_rounded(kept, partner(sent, bit))


def rejoin(values, bit):
    other = partner(values, bit)
    lower = upper_half(bit) == 0
    return jnp.concatenate(
        [jnp.where(lower, values, other), jnp.where(lower, other, values)], axis=0
    )


def bit_order(swapped):
    bits = list(range(int(math.log2(lax.axis_size("replica")))))
    if swapped and len(bits) > 2:
        bits[1], bits[2] = bits[2], bits[1]
    return bits


def replica_sum(values, swapped, stages):
    bits = bit_order(swapped)
    steps = [(halve, bit) for bit in bits] + [(rejoin, bit) for bit in reversed(bits)]
    for i, (step, bit) in enumerate(steps):
        if 2 <= i < len(stages) + 2:
            values, _ = lax.optimization_barrier((values, stages[i - 2]))
        values = step(values, bit)
    return values


def local(
    tokens,
    seq_lens,
    cotangent,
    norm1_gain,
    w_query,
    key_weight,
    value_weight,
    w_output,
    norm2_gain,
    w_gate,
    w_up,
    w_down,
):
    token_count, width = tokens.shape
    group = lax.axis_index("group")
    half_width = w_query.shape[0]
    query_width = w_query.shape[1]
    key_width = key_weight.shape[1]
    gains_mine = jnp.stack([norm1_gain, norm2_gain])
    group_size = lax.axis_size("group")
    gains = in_group_order(
        [gains_mine] + [from_member(gains_mine, k) for k in range(1, group_size)], 1
    )
    gain_one, gain_two = gains[0], gains[1]
    qkv_weight = gather_rows(jnp.concatenate([w_query, key_weight, value_weight], axis=1))
    out_weight = gather_rows(w_output)
    d_out = cotangent.astype(jnp.float32)
    d_out_pair = group_tokens(cotangent)

    cosine_table, sine_table, visible = sequence_tables(seq_lens[0], token_count)
    resid_in = tokens.astype(jnp.float32)
    normed_one, inv_rms_one = rms_scale(resid_in, gain_one)
    qkv = matrix_product(normed_one, qkv_weight)
    query_rotated = apply_rotary(
        qkv[:, :query_width].reshape(token_count, QUERY_HEADS, HEAD_SIZE), cosine_table, sine_table
    ).astype(jnp.bfloat16)
    key_rotated = apply_rotary(
        qkv[:, query_width : query_width + key_width].reshape(
            token_count, KEY_VALUE_HEADS, HEAD_SIZE
        ),
        cosine_table,
        sine_table,
    ).astype(jnp.bfloat16)
    value_rows = (
        qkv[:, query_width + key_width :]
        .astype(jnp.bfloat16)
        .reshape(token_count, KEY_VALUE_HEADS, HEAD_SIZE)
    )
    attn_mix, log_total = attention(query_rotated, key_rotated, value_rows, visible)
    resid_mid = resid_in + matrix_product(attn_mix, out_weight)
    normed_two, inv_rms_two = rms_scale(resid_mid, gain_two)

    normed_pair = group_tokens(normed_two)
    gate_pre = matrix_product(normed_pair, w_gate)
    up_pre = matrix_product(normed_pair, w_up)
    sigma = jax.nn.sigmoid(gate_pre)
    hidden = (gate_pre * sigma * up_pre).astype(jnp.bfloat16)
    grad_down = left_t_product(hidden, d_out_pair).astype(jnp.bfloat16)
    d_hidden = right_t_product(d_out_pair, w_down)
    d_gate = (d_hidden * up_pre * sigma * (1.0 + gate_pre * (1.0 - sigma))).astype(jnp.bfloat16)
    d_up = (d_hidden * gate_pre * sigma).astype(jnp.bfloat16)
    d_normed_part = right_t_product(d_gate, w_gate) + right_t_product(d_up, w_up)
    d_normed_two = group_scatter_sum(d_normed_part, token_count)
    grad_gate = left_t_product(normed_pair, d_gate).astype(jnp.bfloat16)
    grad_up = left_t_product(normed_pair, d_up).astype(jnp.bfloat16)
    down_part = matrix_product(hidden, w_down)
    layer_out = (resid_mid + group_scatter_sum(down_part, token_count)).astype(jnp.bfloat16)

    d_resid_part, grad_gain_two = rms_back(d_normed_two, resid_mid, inv_rms_two, gain_two)
    d_resid_mid = d_out + d_resid_part
    d_mid_b = d_resid_mid.astype(jnp.bfloat16)
    grad_output = left_t_product(attn_mix, d_mid_b)
    d_mix = right_t_product(d_mid_b, out_weight).astype(jnp.bfloat16)
    d_query, d_key, d_value = attention_back(
        query_rotated, key_rotated, value_rows, attn_mix, d_mix, log_total, visible
    )
    d_qkv = jnp.concatenate(
        [
            rotary_backward(d_query, cosine_table, sine_table)
            .reshape(token_count, query_width)
            .astype(jnp.bfloat16),
            rotary_backward(d_key, cosine_table, sine_table)
            .reshape(token_count, key_width)
            .astype(jnp.bfloat16),
            d_value.reshape(token_count, key_width).astype(jnp.bfloat16),
        ],
        axis=1,
    )
    grad_qkv = left_t_product(normed_one, d_qkv)
    d_normed_one = right_t_product(d_qkv, qkv_weight)
    d_resid_first, grad_gain_one = rms_back(d_normed_one, resid_in, inv_rms_one, gain_one)
    tokens_grad = d_resid_mid + d_resid_first

    columns = query_width + 2 * key_width + width
    attn_grads = jnp.concatenate([grad_qkv, grad_output], axis=1).astype(jnp.bfloat16)
    replicas = lax.axis_size("replica")
    extra = replicas - half_width % replicas
    gain_rows = jnp.stack([grad_gain_one, grad_gain_two]).reshape(2, group_size, half_width)
    gain_rows = gain_rows.transpose(1, 0, 2).reshape(group_size, 1, 2 * half_width)
    gain_rows = jnp.pad(
        gain_rows.astype(jnp.bfloat16), ((0, 0), (0, extra - 1), (0, columns - 2 * half_width))
    )
    blocks = jnp.concatenate(
        [attn_grads.reshape(group_size, half_width, columns), gain_rows], axis=1
    )
    blocks = halve(blocks, 0, axis=1)
    stages = [blocks]
    summed = lax.dynamic_index_in_dim(blocks, group, axis=0, keepdims=False)
    for k in range(1, group_size):
        owner = lax.rem(group + k, group_size)
        part = lax.dynamic_index_in_dim(blocks, owner, axis=0, keepdims=False)
        summed = add_rounded(summed, to_member(part, k))
    stages.append(summed)
    later = bit_order(True)[1:]
    for bit in later:
        summed = halve(summed, bit)
        stages.append(summed)
    for bit in reversed(later):
        summed = rejoin(summed, bit)
        stages.append(summed)
    sum_attn = rejoin(summed, 0)
    sum_down = replica_sum(grad_down, False, stages)
    sum_gate = replica_sum(grad_gate, False, stages)
    sum_up = replica_sum(grad_up, True, stages)

    factor = 1.0 / math.sqrt(
        float(token_count * lax.axis_size("group") * lax.axis_size("replica"))
    )

    def scaled(values):
        return values.astype(jnp.float32) * factor

    gain_sums = scaled(sum_attn[half_width])
    sum_attn = scaled(sum_attn[:half_width])
    return (
        layer_out,
        tokens_grad,
        gain_sums[:half_width],
        sum_attn[:, :query_width],
        sum_attn[:, query_width : query_width + key_width],
        sum_attn[:, query_width + key_width : query_width + 2 * key_width],
        sum_attn[:, query_width + 2 * key_width :],
        gain_sums[half_width : 2 * half_width],
        scaled(sum_gate),
        scaled(sum_up),
        scaled(sum_down),
    )


def solution(mesh):
    in_specs = (
        P(("group", "replica"), None),
        P(("group", "replica"), None),
        P(("group", "replica"), None),
        P("group"),
        P("group", None),
        P("group", None),
        P("group", None),
        P("group", None),
        P("group"),
        P(None, "group"),
        P(None, "group"),
        P("group", None),
    )
    out_specs = (
        P(("group", "replica"), None),
        P(("group", "replica"), None),
        P("group"),
        P("group", None),
        P("group", None),
        P("group", None),
        P("group", None),
        P("group"),
        P(None, "group"),
        P(None, "group"),
        P("group", None),
    )
    return jax.shard_map(local, mesh=mesh, in_specs=in_specs, out_specs=out_specs, check_vma=False)
```
